32 devices in a mesh: groups: 2 (over y), seq: 4 (over z), mp: 2 (over x), section: 2 (over core).
Axes of the slice: x: 2, y: 2, z: 4, core: 2. Of those that a mesh axis runs over, the one named last changes fastest.
Arguments:
- features: bfloat16 [4, 512, 8192], P(('groups', 'section'), 'mp', 'seq'), parts along dimension 0, may hold values from -6 to 6
- alpha: float32 [512], P('mp'), may hold values from 0.5 to 2
- conv_weight: bfloat16 [1024, 32, 16], P('mp'), may hold values from -0.25 to 0.25
- qkv_weight: bfloat16 [1024, 3, 1024], P(None, None, 'mp'), may hold values from -1 to 1
- readout: float32 [1024], P('mp'), may hold values from -4 to 4
- offsets: int32 [4], P(('groups', 'section')), parts along dimension 0, may hold values from 0 to 14479
- pairs: int32 [8, 2], P('groups'), parts along dimension 0, may hold values from 0 to 1
- labels: int32 [8], P('groups'), parts along dimension 0, may hold values from 0 to 1
Outputs:
- grads: bfloat16 [3, 4, 1024, 1024], P(None, ('groups', 'section'), 'seq', 'mp'), parts along dimension 1
- rewards: float32 [4], P('groups'), parts along dimension 0
- loss: float32 [2], P('groups'), parts along dimension 0
The draws below stay inside these ranges and needn't reach their ends.
There are 2 independent parts, one for each index of `groups`. The reference program is written for one: setup_inputs(seed, part) draws one part's arguments, and reference() takes and returns one part's arrays. A program takes and returns all parts, laid end to end along the dimension named above; an argument that names none is the same for every part. Nothing has to cross between parts.
All inputs are finite; a program needn't handle non-finite values.
Results may differ from the reference program's by a relative error of at most 0.017.
Values may be sent and summed in bfloat16 or wider, within the bound.
A program may use at most 64 MiB of HBM per device.

```python
import math
import jax
import jax.numpy as jnp
from jax import lax

D = 1024
HEADS = 16
HD = 64
CIN = 512
GROUPS = 16
STRIDE = 8
KERN = 16
CLIP = 15503
FR_DEV = 256
CANDS = 2
FR = 1024
SAMP = 8192
PAIRS = 4
N_SEQ = 4


def draw_qkv_weight(key, part):
    first = jax.random.fold_in(key, 0)
    base = jnp.clip(jax.random.normal(first, (D, 3, D), jnp.float32), -5.0, 5.0)
    weight = base * jnp.sqrt(3.0 / D)
    return jnp.clip(weight, -1.0, 1.0).astype(jnp.bfloat16)


def with_ends(values, key, low, high):
    index_at = [jax.random.randint(jax.random.fold_in(key, axis), (), 0, length) for axis, length in enumerate(values.shape)]
    widest = values.shape.index(max(values.shape))
    neighbour = index_at[:widest] + [(index_at[widest] + 1) % values.shape[widest]] + index_at[widest + 1:]
    return values.at[tuple(index_at)].set(low).at[tuple(neighbour)].set(high)


def block_scale(rng, extent, shards, low, largest):
    gain = 1.0
    for dim, parts in shards:
        heights = jax.random.uniform(jax.random.fold_in(jax.random.fold_in(rng, 6), dim), (parts,), jnp.float32, low / len(shards), largest / len(shards))
        gain = gain * jnp.repeat(jnp.exp(heights), extent[dim] // parts).reshape((-1,) + (1,) * (len(extent) - 1 - dim))
    return gain


def bell_draw(rng, dims, deviation, bound, pieces=(), kind=jnp.bfloat16):
    level = block_scale(rng, dims, pieces, -0.22, 0.18) if pieces else 1.0
    drawn = jax.random.normal(rng, dims, jnp.float32) * deviation * level
    return jnp.minimum(jnp.maximum(drawn, -bound), bound).astype(kind)


def setup_inputs(seed: int = 0, part: int = 0) -> dict:
    key_list = jax.random.split(jax.random.key(seed), 9)
    own_keys = jax.random.split(jax.random.fold_in(key_list[8], part), 9)
    features = bell_draw(own_keys[0], (CANDS, CIN, SAMP), 1.0, 6.0, ((0, 2), (1, 2), (2, 4)))
    alpha = jnp.clip(jnp.exp(math.log(2.0) - 1.3862944 * jax.random.uniform(key_list[1], (CIN,), jnp.float32) ** block_scale(key_list[1], (CIN,), ((0, 2),), -0.2, 0.2)), 0.5, 2.0)
    conv_weight = bell_draw(key_list[2], (D, CIN // GROUPS, KERN), (CIN // GROUPS * KERN) ** -0.5, 0.25, ((0, 2),))
    qkv_weight = draw_qkv_weight(jax.random.fold_in(key_list[8], 71), part)
    readout = bell_draw(key_list[4], (D,), 0.25, 4.0, ((0, 2),), jnp.float32)
    offsets = jax.random.randint(own_keys[5], (CANDS,), 0, CLIP - FR + 1).astype(jnp.int32)
    pairs = with_ends(jax.random.randint(own_keys[6], (PAIRS, 2), 0, CANDS), jax.random.fold_in(own_keys[6], 1), 0, CANDS - 1).astype(jnp.int32)
    labels = with_ends(jax.random.randint(own_keys[7], (PAIRS,), 0, 2), jax.random.fold_in(own_keys[7], 1), 0, 1).astype(jnp.int32)
    return dict(features=features, alpha=alpha, conv_weight=conv_weight, qkv_weight=qkv_weight, readout=readout, offsets=offsets, pairs=pairs, labels=labels)


EPS = 1e-06
BASE = 10000.0

def position_table(positions, feature_ids, width):
    pair_ids = (feature_ids // 2).astype(jnp.float32)
    freqs = jnp.exp(pair_ids * (-2.0 * math.log(BASE) / width))
    angle = positions.astype(jnp.float32)[..., None] * freqs
    return jnp.where(feature_ids % 2 == 0, jnp.sin(angle), jnp.cos(angle))

def rounded(value):
    return lax.optimization_barrier(value.astype(jnp.bfloat16)).astype(jnp.float32)

def heads_first(value):
    return value.reshape(CANDS, FR, HEADS, HD).transpose(2, 0, 1, 3)

def heads_back(value):
    return value.transpose(1, 2, 0, 3).reshape(CANDS, FR, D)

def reference(features, alpha, conv_weight, qkv_weight, readout, offsets, pairs, labels):
    f32 = jnp.float32
    raw = features.astype(f32)
    slope = alpha.astype(f32)[None, :, None]
    act = (raw + jnp.sin(slope * raw) ** 2 / slope).astype(jnp.bfloat16)
    half = STRIDE // 2
    padded = jnp.pad(act, ((0, 0), (0, 0), (half, half)))
    per_group = CIN // GROUPS
    blocks = padded.reshape(CANDS, GROUPS, per_group, FR + 1, STRIDE).transpose(0, 1, 3, 2, 4)
    patches = jnp.concatenate([blocks[:, :, :-1], blocks[:, :, 1:]], axis=-1).reshape(CANDS, GROUPS, FR, per_group * KERN)
    kernel = conv_weight.reshape(GROUPS, D // GROUPS, per_group * KERN)
    frames = jnp.einsum('cgfk,gok->cfgo', patches.astype(f32), kernel.astype(f32)).reshape(CANDS, FR, D)
    positions = offsets.astype(jnp.int32)[:, None] + jnp.arange(FR, dtype=jnp.int32)[None, :]
    resid = rounded(frames + position_table(positions, jnp.arange(D, dtype=jnp.int32), D))
    squares = lax.optimization_barrier(jnp.mean(resid * resid, axis=-1))
    projected = jnp.einsum('cfd,dtk->cftk', resid, qkv_weight.astype(f32))
    qkv = rounded(projected * lax.rsqrt(squares + EPS)[:, :, None, None])
    query = heads_first(qkv[:, :, 0])
    keys = heads_first(qkv[:, :, 1])
    values = heads_first(qkv[:, :, 2])
    scale = 1.0 / math.sqrt(HD)

    def probabilities(qpart, kpart):
        score = jnp.einsum('cqe,cke->cqk', qpart, kpart) * scale
        peak = lax.optimization_barrier(jnp.max(score, axis=-1, keepdims=True))
        weight = jnp.exp(score - peak)
        return weight / lax.optimization_barrier(jnp.sum(weight, axis=-1, keepdims=True))

    def forward_head(item):
        qpart, kpart, vpart = item
        prob = rounded(probabilities(qpart, kpart))
        return jnp.einsum('cqk,cke->cqe', prob, vpart)
    attended_heads = lax.map(forward_head, (query, keys, values))
    attended = heads_back(attended_heads)
    gate = jax.nn.sigmoid(resid)
    read = readout.astype(f32)
    rewards = lax.optimization_barrier(jnp.sum(attended * gate * read, axis=(1, 2))) / math.sqrt(FR)
    chosen = (pairs[:, :, None] == jnp.arange(CANDS, dtype=jnp.int32)[None, None, :]).astype(f32)
    paired = lax.optimization_barrier(jnp.sum(chosen * rewards[None, None, :], axis=-1))
    margin = paired[:, 0] - paired[:, 1]
    target = labels.astype(f32)
    loss = jnp.sum(jax.nn.softplus(margin) - target * margin)
    coeff = jax.nn.sigmoid(margin) - target
    reward_grad = lax.optimization_barrier(jnp.sum(coeff[:, None] * (chosen[:, 0] - chosen[:, 1]), axis=0))
    upstream = rounded(reward_grad[:, None, None] * read * gate)
    upstream_heads = heads_first(upstream)
    delta = lax.optimization_barrier(jnp.sum(upstream_heads * attended_heads, axis=-1))

    def backward_head(item):
        qpart, kpart, vpart, uppart, dpart = item
        prob = probabilities(qpart, kpart)
        prob_low = rounded(prob)
        dprob = jnp.einsum('cqe,cke->cqk', uppart, vpart)
        dscore = rounded(prob * (dprob - dpart[..., None]))
        grad_q = jnp.einsum('cqk,cke->cqe', dscore, kpart) * scale
        q_blocks = qpart.reshape(CANDS, N_SEQ, FR_DEV, HD)
        up_blocks = uppart.reshape(CANDS, N_SEQ, FR_DEV, HD)
        ds_blocks = dscore.reshape(CANDS, N_SEQ, FR_DEV, FR)
        p_blocks = prob_low.reshape(CANDS, N_SEQ, FR_DEV, FR)
        grad_k = lax.optimization_barrier(jnp.sum(rounded(jnp.einsum('cbqk,cbqe->cbke', ds_blocks, q_blocks) * scale), axis=1))
        grad_v = lax.optimization_barrier(jnp.sum(rounded(jnp.einsum('cbqk,cbqe->cbke', p_blocks, up_blocks)), axis=1))
        return (grad_q, grad_k, grad_v)
    grad_q, grad_k, grad_v = lax.map(backward_head, (query, keys, values, upstream_heads, delta))
    grads = jnp.stack([heads_back(grad_q), heads_back(grad_k), heads_back(grad_v)], axis=0).astype(jnp.bfloat16)
    return (grads, rewards, loss.reshape(1))
```

```python
import math

import jax
import jax.numpy as jnp
import numpy as np
from jax import lax
from jax.experimental import pallas as pl
from jax.experimental.pallas import tpu as pltpu
from jax.sharding import PartitionSpec as P

D = 1024
HD = 64


EPS = 1e-06
BASE = 10000.0


def padded_2(block, sides, width):
    for axis, dim in sides:
        count = lax.axis_size(axis)
        forward = [(i, i + 1) for i in range(count - 1)]
        backward = [(target, source) for source, target in forward]
        low = lax.ppermute(
            lax.slice_in_dim(block, block.shape[dim] - width, None, axis=dim), axis, forward
        )
        high = lax.ppermute(lax.slice_in_dim(block, 0, width, axis=dim), axis, backward)
        block = jnp.concatenate([low, block, high], axis=dim)
    return block


def position_table(positions, feature_ids, width):
    pair_ids = (feature_ids // 2).astype(jnp.float32)
    freqs = jnp.exp(pair_ids * (-2.0 * math.log(BASE) / width))
    angle = positions.astype(jnp.float32)[..., None] * freqs
    return jnp.where(feature_ids % 2 == 0, jnp.sin(angle), jnp.cos(angle))


def local(features, alpha, conv_weight, qkv_weight, readout, offsets, pairs, labels):
    f32 = jnp.float32
    bf16 = jnp.bfloat16
    cand, chans, samples = features.shape
    local_width = conv_weight.shape[0]
    per_group = conv_weight.shape[1]
    kern = conv_weight.shape[2]
    stride = kern // 2
    frames_dev = samples // stride
    groups_here = chans // per_group
    heads_here = local_width // HD
    raw = features.astype(f32)
    slope = alpha[None, :, None]
    act = (raw + jnp.sin(slope * raw) ** 2 / slope).astype(bf16)
    padded = padded_2(act, (("seq", 2),), stride // 2)
    blocks = padded.reshape(cand, groups_here, per_group, frames_dev + 1, stride).transpose(
        0, 1, 3, 2, 4
    )
    patches = jnp.concatenate([blocks[:, :, :-1], blocks[:, :, 1:]], axis=-1).reshape(
        cand, groups_here, frames_dev, per_group * kern
    )
    kernel = conv_weight.reshape(groups_here, local_width // groups_here, per_group * kern)
    frames = jnp.einsum("cgfk,gok->cfgo", patches, kernel, preferred_element_type=f32).reshape(
        cand, frames_dev, local_width
    )
    slice_id = lax.axis_index("seq")
    part_id = lax.axis_index("mp")
    positions = (
        offsets[:, None] + slice_id * frames_dev + jnp.arange(frames_dev, dtype=jnp.int32)[None, :]
    )
    feature_ids = part_id * local_width + jnp.arange(local_width, dtype=jnp.int32)
    resid = (frames + position_table(positions, feature_ids, D)).astype(bf16)
    whole = lax.all_gather(resid, "mp", axis=2, tiled=True)
    squares = jnp.mean(jnp.square(whole.astype(f32)), axis=-1)
    projected = jnp.einsum("cfd,dtk->cftk", whole, qkv_weight, preferred_element_type=f32)
    qkv = (projected * lax.rsqrt(squares + EPS)[:, :, None, None]).astype(bf16)
    query = qkv[:, :, 0]
    keys, values = (
        lax.all_gather(qkv[:, :, 1], "seq", axis=1, tiled=True),
        lax.all_gather(qkv[:, :, 2], "seq", axis=1, tiled=True),
    )
    total = keys.shape[1]
    block = min(512, total)
    count_blocks = total // block
    scale = 1.0 / math.sqrt(HD)
    query4 = query.reshape(cand, frames_dev, heads_here, HD)

    def key_slice(source, start, size):
        return lax.dynamic_slice_in_dim(source, start, size, 1).reshape(cand, size, heads_here, HD)

    def scores_for(start, size):
        return (
            jnp.einsum(
                "cfhe,ckhe->chfk", query4, key_slice(keys, start, size), preferred_element_type=f32
            )
            * scale
        )

    def stat_step(carry, index):
        peak_now, mass_now = carry
        score = scores_for(index * block, block)
        fresh = jnp.maximum(peak_now, jnp.max(score, axis=-1))
        mass_now = mass_now * jnp.exp(peak_now - fresh) + jnp.sum(
            jnp.exp(score - fresh[..., None]), axis=-1
        )
        return ((fresh, mass_now), None)

    start_peak = jnp.full((cand, heads_here, frames_dev), -jnp.inf, f32)
    (peak, mass), _ = lax.scan(
        stat_step, (start_peak, jnp.zeros_like(start_peak)), jnp.arange(count_blocks)
    )

    def weights_for(start, size):
        return jnp.exp(scores_for(start, size) - peak[..., None]) / mass[..., None]

    def out_step(running, index):
        start = index * block
        prob = weights_for(start, block).astype(bf16)
        running = running + jnp.einsum(
            "chfk,ckhe->cfhe", prob, key_slice(values, start, block), preferred_element_type=f32
        )
        return (running, None)

    attended4, _ = lax.scan(
        out_step, jnp.zeros((cand, frames_dev, heads_here, HD), f32), jnp.arange(count_blocks)
    )
    attended = attended4.reshape(cand, frames_dev, local_width)
    gate = jax.nn.sigmoid(lax.optimization_barrier(resid).astype(f32))
    section_id = lax.axis_index("section")
    all_cands = cand * lax.axis_size("section")
    owner = (
        jnp.arange(all_cands, dtype=jnp.int32)[None, :]
        == (section_id * cand + jnp.arange(cand, dtype=jnp.int32))[:, None]
    ).astype(f32)
    partial_rewards = jnp.sum(attended * gate * readout, axis=(1, 2)) / math.sqrt(total)
    rewards = lax.psum(jnp.sum(owner * partial_rewards[:, None], axis=0), ("seq", "mp", "section"))
    chosen = (pairs[:, :, None] == jnp.arange(all_cands, dtype=jnp.int32)[None, None, :]).astype(
        f32
    )
    paired = jnp.sum(chosen * rewards[None, None, :], axis=-1)
    margin = paired[:, 0] - paired[:, 1]
    target = labels.astype(f32)
    loss = jnp.sum(jax.nn.softplus(margin) - target * margin)
    coeff = jax.nn.sigmoid(margin) - target
    reward_grad = jnp.sum(coeff[:, None] * (chosen[:, 0] - chosen[:, 1]), axis=0)
    own_grad = jnp.sum(owner * reward_grad[None, :], axis=1)
    upstream = (own_grad[:, None, None] * readout * gate).astype(bf16)
    upstream4 = upstream.reshape(cand, frames_dev, heads_here, HD)
    delta = jnp.sum(upstream4.astype(f32) * attended4, axis=-1).transpose(0, 2, 1)

    def backward_block(start, size):
        prob = weights_for(start, size)
        prob_low = prob.astype(bf16)
        dprob = jnp.einsum(
            "cfhe,ckhe->chfk", upstream4, key_slice(values, start, size), preferred_element_type=f32
        )
        dscore = (prob * (dprob - delta[..., None])).astype(bf16)
        dquery = (
            jnp.einsum(
                "chfk,ckhe->cfhe", dscore, key_slice(keys, start, size), preferred_element_type=f32
            )
            * scale
        )
        dkey = jnp.einsum("chfk,cfhe->kche", dscore, query4, preferred_element_type=f32) * scale
        dvalue = jnp.einsum("chfk,cfhe->kche", prob_low, upstream4, preferred_element_type=f32)
        term = jnp.concatenate(
            [dkey.reshape(size, cand, local_width), dvalue.reshape(size, cand, local_width)],
            axis=-1,
        )
        return (dquery, term)

    zero_query = jnp.zeros((cand, frames_dev, heads_here, HD), f32)

    def grad_step(running, index):
        dquery, term = backward_block(index * block, block)
        return (running + dquery, term.astype(bf16))

    grad_query, stored = lax.scan(grad_step, zero_query, jnp.arange(count_blocks))
    stacked = stored.reshape(total, cand, 2 * local_width)
    summed = lax.psum_scatter(
        stacked.astype(f32).astype(jnp.bfloat16), "seq", scatter_dimension=0, tiled=True
    ).astype(jnp.float32)
    grad_key = summed[:, :, :local_width].transpose(1, 0, 2)
    grad_value = summed[:, :, local_width:].transpose(1, 0, 2)
    grads = jnp.stack(
        [grad_query.reshape(cand, frames_dev, local_width), grad_key, grad_value], axis=0
    ).astype(bf16)
    return (grads, rewards, loss.reshape(1))


PI_PARTS = (3.140625, 0.0009670257568359375, 6.2771141529083251953e-07, 1.2154201256553420762e-10)
SIN_COEFFS = (-1.0 / 6, 1.0 / 120, -1.0 / 5040, 1.0 / 362880, -1.0 / 39916800)


def reduced_sin(angle, turns, parts):
    for part in PI_PARTS[:parts]:
        angle = angle - turns * part
    square = angle * angle
    poly = jnp.full_like(square, SIN_COEFFS[-1])
    for coeff in SIN_COEFFS[-2::-1]:
        poly = poly * square + coeff
    return angle + angle * square * poly


def snake(raw, slope, inverse):
    angle = slope * raw
    sine = reduced_sin(angle, jnp.round(angle * (1.0 / math.pi)), 3)
    return (raw + sine * sine * inverse).astype(jnp.bfloat16)


def nn(a, b):
    return jnp.dot(a, b, preferred_element_type=jnp.float32)


def nt(a, b):
    return lax.dot_general(a, b, (((1,), (1,)), ((), ())), preferred_element_type=jnp.float32)


def fused_kernel(n_seq, n_mp, n_sec):
    f32 = jnp.float32
    bf16 = jnp.bfloat16

    def kernel(
        feats, alpha, conv_w, qkv_w, readout, freqs, offsets, pairs, labels,
        grads, rewards_out, loss_out,
        halo, act0, act1, conv_f, conv_b, patches, weights, whole, resid_out, resid_in,
        qkv_out, qkv_in, prob, up_m, q_m, delta, gq_sum, reward_slots, grad_out,
        halo_sem, mp_sem, weight_sem, resid_sem, qkv_sem, reward_sem, grad_sem,
    ):
        me = lax.axis_index("seq")
        part = lax.axis_index("mp")
        sec = lax.axis_index("section")
        other = 1 - part
        chans, samples = feats.shape
        taps = conv_w.shape[1]
        per_group = conv_w.shape[0]
        width = conv_w.shape[2]
        stride = taps // 2
        fr = samples // stride
        cols = width // n_seq
        total = fr * n_seq

        def remote(src, dst, sems, send, recv, **where):
            return pltpu.make_async_remote_copy(
                src_ref=src, dst_ref=dst, send_sem=sems.at[0].at[send], recv_sem=sems.at[1].at[recv],
                device_id=where, device_id_type=pl.DeviceIdType.MESH,
            )

        weight_copy = pltpu.make_async_copy(qkv_w, weights, weight_sem)
        weight_copy.start()
        barrier = pltpu.get_barrier_semaphore()
        peers = [
            (a, b, c) for a in range(n_seq) for b in range(n_mp) for c in range(n_sec) if (a, b, c) != (0, 0, 0)
        ]

        def peer(step):
            return dict(
                seq=lax.rem(me + step[0], n_seq),
                mp=lax.rem(part + step[1], n_mp),
                section=lax.rem(sec + step[2], n_sec),
            )

        for step in peers:
            pl.semaphore_signal(barrier, inc=1, device_id=peer(step), device_id_type=pl.DeviceIdType.MESH)
        pl.semaphore_wait(barrier, len(peers))

        to_right = remote(feats.at[:, samples - 128 : samples], halo.at[0], halo_sem, 0, 0, seq=lax.rem(me + 1, n_seq))
        to_left = remote(feats.at[:, 0:128], halo.at[1], halo_sem, 1, 1, seq=lax.rem(me + n_seq - 1, n_seq))

        @pl.when(me < n_seq - 1)
        def _():
            to_right.start()

        @pl.when(me > 0)
        def _():
            to_left.start()

        slope = alpha[...]
        inverse = 1.0 / slope

        def put_act(row, block):
            act0[pl.ds(row, block.shape[0]), :] = block[:, :128]
            act1[pl.ds(row, block.shape[0]), :] = block[:, 128:]

        def act_step(i, carry):
            raw = feats[:, pl.ds(pl.multiple_of(i * 256, 256), 256)].astype(f32).T
            put_act(pl.multiple_of(8 + i * 256, 8), snake(raw, slope, inverse).astype(f32))
            return carry

        lax.fori_loop(0, samples // 256, act_step, 0)

        for j in range(width // 128):
            conv_f[j] = conv_w[:, :, j * 128 : (j + 1) * 128].astype(f32).reshape(per_group * taps, 128)
        group_out = width // (chans // per_group)
        for j in range(width // 128):
            rows = lax.broadcasted_iota(jnp.int32, (chans, 128), 0) // per_group
            outs = (lax.broadcasted_iota(jnp.int32, (chans, 128), 1) + j * 128) // group_out
            for t in range(taps):
                tap = conv_f.at[j][pl.ds(t, per_group, stride=taps), :]
                tiled = jnp.concatenate([tap] * (chans // per_group), axis=0)
                conv_b[t * chans : (t + 1) * chans, j * 128 : (j + 1) * 128] = jnp.where(rows == outs, tiled, 0.0).astype(bf16)

        feature = lax.broadcasted_iota(jnp.int32, (1, width), 1)
        odd = (feature - 2 * (feature // 2)).astype(f32)
        spots = (offsets[0] + me * fr + lax.broadcasted_iota(jnp.int32, (fr, 1), 0)).astype(f32)
        angle = spots * freqs[:, pl.ds(pl.multiple_of(part * width, 128), width)]
        whole_turns = jnp.round(angle * (1.0 / math.pi) - 0.5 * odd)
        sine = reduced_sin(angle, whole_turns + 0.5 * odd, 4)
        signed = whole_turns + odd
        parity = signed - 2.0 * jnp.floor(signed * 0.5)
        table = sine * (1.0 - 2.0 * parity)

        @pl.when(me < n_seq - 1)
        def _():
            to_right.wait_send()
            to_left.wait_recv()
            put_act(8 + samples, snake(halo[1].astype(f32).T[:8], slope, inverse).astype(f32))

        @pl.when(me == n_seq - 1)
        def _():
            put_act(8 + samples, jnp.zeros((8, chans), f32))

        @pl.when(me > 0)
        def _():
            to_left.wait_send()
            to_right.wait_recv()
            put_act(0, snake(halo[0].astype(f32).T[120:], slope, inverse).astype(f32))

        @pl.when(me == 0)
        def _():
            put_act(0, jnp.zeros((8, chans), f32))

        for t in range(taps):
            first = 8 - stride // 2 + t
            patches[:, t * chans : t * chans + 128] = act0[pl.ds(first, fr, stride=stride), :].astype(bf16)
            patches[:, t * chans + 128 : (t + 1) * chans] = act1[pl.ds(first, fr, stride=stride), :].astype(bf16)
        resid = (nn(patches[...], conv_b[...]) + table).astype(bf16)

        whole[part] = resid
        to_mp = remote(whole.at[part], whole.at[part], mp_sem, 0, 0, mp=other)
        to_mp.start()
        for z in range(n_seq):
            resid_out[z] = resid[:, z * cols : (z + 1) * cols]
        resid_in[me] = resid_out[me]
        sent = []
        for d in range(1, n_seq):
            z = lax.rem(me + d, n_seq)
            copy = remote(resid_out.at[z], resid_in.at[me], resid_sem, z, me, seq=z)
            copy.start()
            sent.append(copy)
        wide = resid.astype(f32)
        squares = jnp.sum(wide * wide, axis=1, keepdims=True)
        own_rows = pl.ds(pl.multiple_of(part * width, 128), width)
        other_rows = pl.ds(pl.multiple_of(other * width, 128), width)
        weight_copy.wait()
        halves = [nn(resid, weights[t, own_rows, :]) for t in range(3)]
        from_mp = remote(whole.at[other], whole.at[other], mp_sem, 0, 0, mp=other)
        from_mp.wait_recv()
        rest = whole[other]
        wide = rest.astype(f32)
        squares = squares + jnp.sum(wide * wide, axis=1, keepdims=True)
        norm = lax.rsqrt(squares * (1.0 / (width * n_mp)) + EPS)
        for t in (1, 2, 0):
            value = ((halves[t] + nn(rest, weights[t, other_rows, :])) * norm).astype(bf16)
            if t == 0:
                value = value * jnp.asarray(1.0 / math.sqrt(HD), bf16)
            for z in range(n_seq):
                qkv_out[t, z] = value[:, z * cols : (z + 1) * cols]
            qkv_in[t, me] = qkv_out[t, me]
            for d in range(1, n_seq):
                z = lax.rem(me + d, n_seq)
                copy = remote(qkv_out.at[t, z], qkv_in.at[t, me], qkv_sem.at[t], z, me, seq=z)
                copy.start()
                sent.append(copy)

        def arrive(ref, sems):
            for d in range(1, n_seq):
                z = lax.rem(me + d, n_seq)
                remote(ref.at[z], ref.at[z], sems, z, z, seq=z).wait_recv()

        heads = cols // HD
        row_head = lax.broadcasted_iota(jnp.int32, (cols, 1), 0) // HD
        lane_head = lax.broadcasted_iota(jnp.int32, (1, cols), 1) // HD

        def rows_of(value, h):
            return jnp.where(row_head == h, value, jnp.zeros_like(value))

        def lanes_of(value, h):
            return jnp.where(lane_head == h, value, jnp.zeros_like(value))

        def flipped(value):
            return value.astype(f32).T.astype(bf16)

        arrive(resid_in, resid_sem)
        read = jnp.broadcast_to(readout[pl.ds(me, 1), :], (cols, cols)).T[:, :1]
        for z in range(n_seq):
            up = jax.nn.sigmoid(resid_in[z].astype(f32).T) * read
            gq_sum[:, z * fr : (z + 1) * fr] = up
            for h in range(heads):
                up_m[h, :, z * fr : (z + 1) * fr] = rows_of(up, h).astype(bf16)
        for t in (1, 2, 0):
            arrive(qkv_in.at[t], qkv_sem.at[t])

        keys = qkv_in[1].reshape(total, cols)
        values_t = flipped(qkv_in[2].reshape(total, cols))
        for h in range(heads):
            q_m[h] = lanes_of(qkv_in[0].reshape(total, cols), h)
        values_h = [rows_of(values_t, h) for h in range(heads)]

        def forward(c, carry):
            chunk = pl.ds(pl.multiple_of(c * fr, fr), fr)
            attended = jnp.zeros((cols, fr), f32)
            for h in range(heads):
                score = nt(keys, q_m[h, chunk, :])
                weight = jnp.exp(score - jnp.max(score, axis=0, keepdims=True))
                share = weight * (1.0 / jnp.sum(weight, axis=0, keepdims=True))
                prob[h, :, chunk] = share
                out = nn(values_h[h], share.astype(bf16))
                delta[h : h + 1, chunk] = jnp.sum(out * up_m[h, :, chunk].astype(f32), axis=0, keepdims=True)
                attended = attended + out
            return carry + attended * gq_sum[:, chunk]

        reward = lax.fori_loop(0, n_seq, forward, jnp.zeros((cols, fr), f32))
        own = (me * n_mp + part) * n_sec + sec
        reward_slots[own] = jnp.full((8, 128), jnp.sum(reward), f32)
        for step in peers:
            where = peer(step)
            index = (step[0] * n_mp + step[1]) * n_sec + step[2]
            copy = remote(reward_slots.at[own], reward_slots.at[own], reward_sem, index, own, **where)
            copy.start()
            sent.append(copy)

        gq_sum[...] = jnp.zeros_like(gq_sum)
        gain = None
        for d in list(range(1, n_seq)) + [0]:
            z = lax.rem(me + d, n_seq)
            rows = pl.ds(pl.multiple_of(z * fr, fr), fr)
            key_t = flipped(qkv_in[1, z]) * jnp.asarray(1.0 / math.sqrt(HD), bf16)
            grad_k = jnp.zeros((fr, cols), f32)
            grad_v = jnp.zeros((fr, cols), f32)
            for h in range(heads):
                share = prob[h, rows, :]
                dprob = nn(qkv_in[2, z], up_m[h])
                dscore = (share * (dprob - delta[h : h + 1, :])).astype(bf16)
                grad_k = grad_k + nn(dscore, q_m[h])
                grad_v = grad_v + nt(share.astype(bf16), up_m[h])
                gq_sum[...] += nn(rows_of(key_t, h), dscore)
            if gain is None:
                for step in peers:
                    where = peer(step)
                    index = (where["seq"] * n_mp + where["mp"]) * n_sec + where["section"]
                    remote(reward_slots.at[index], reward_slots.at[index], reward_sem, 0, index, **where).wait_recv()
                rewards = []
                for c in range(n_sec):
                    one = reward_slots[c]
                    for k in range(1, n_seq * n_mp):
                        one = one + reward_slots[k * n_sec + c]
                    one = one * (1.0 / math.sqrt(total))
                    rewards.append(one)
                    rewards_out[c] = jnp.max(one)
                loss = jnp.zeros((8, 128), f32)
                gain = jnp.zeros((8, 128), f32)
                for p in range(labels.shape[0]):
                    picks = [pairs[p, 0], pairs[p, 1]]
                    sides = []
                    for pick in picks:
                        flag = pick.astype(f32)
                        sides.append(rewards[0] * (1.0 - flag) + rewards[1] * flag)
                    margin = sides[0] - sides[1]
                    target = labels[p].astype(f32)
                    loss = loss + jnp.maximum(margin, 0.0) + jnp.log1p(jnp.exp(-jnp.abs(margin))) - target * margin
                    mine = (1 - jnp.abs(picks[0] - sec)) - (1 - jnp.abs(picks[1] - sec))
                    gain = gain + (jax.nn.sigmoid(margin) - target) * mine.astype(f32)
                loss_out[0] = jnp.max(loss)
                gain = gain[:1, :1]
            pieces = ((1, grad_k), (2, grad_v))
            for t, piece in pieces:
                scaled = (piece * gain).astype(bf16)
                if d == 0:
                    grads[t, :, pl.ds(pl.multiple_of(me * cols, cols), cols)] = scaled
                else:
                    grad_out[t, d] = scaled
                    copy = remote(
                        grad_out.at[t, d], grads.at[t, :, pl.ds(pl.multiple_of(me * cols, cols), cols)],
                        grad_sem.at[t], d, me, seq=z,
                    )
                    copy.start()
                    sent.append(copy)
        for d in list(range(1, n_seq)) + [0]:
            z = lax.rem(me + d, n_seq)
            scaled = (gq_sum[:, pl.ds(pl.multiple_of(z * fr, fr), fr)].T * gain).astype(bf16)
            if d == 0:
                grads[0, :, pl.ds(pl.multiple_of(me * cols, cols), cols)] = scaled
            else:
                grad_out[0, d] = scaled
                copy = remote(
                    grad_out.at[0, d], grads.at[0, :, pl.ds(pl.multiple_of(me * cols, cols), cols)],
                    grad_sem.at[0], d, me, seq=z,
                )
                copy.start()
                sent.append(copy)
        for t in (1, 2, 0):
            for d in range(1, n_seq):
                z = lax.rem(me + d, n_seq)
                remote(
                    grad_out.at[t, d], grads.at[t, :, pl.ds(pl.multiple_of(z * cols, cols), cols)],
                    grad_sem.at[t], d, z, seq=z,
                ).wait_recv()
        to_mp.wait_send()
        for copy in sent:
            copy.wait_send()

    return kernel


def fused_local(n_seq, n_mp, n_sec):
    def run(features, alpha, conv_weight, qkv_weight, readout, offsets, pairs, labels):
        f32 = jnp.float32
        bf16 = jnp.bfloat16
        _, chans, samples = features.shape
        width, per_group, taps = conv_weight.shape
        fr = samples // (taps // 2)
        cols = width // n_seq
        total = fr * n_seq
        heads = cols // HD
        powers = np.arange(n_mp * width) // 2 * (-2.0 * math.log(BASE) / (n_mp * width))
        freqs = jnp.asarray(np.exp(powers)[None, :].astype(np.float32))
        vmem = pl.BlockSpec(memory_space=pltpu.VMEM)
        smem = pl.BlockSpec(memory_space=pltpu.SMEM)
        dma = pltpu.SemaphoreType.DMA
        grads, rewards, loss = pl.pallas_call(
            fused_kernel(n_seq, n_mp, n_sec),
            out_shape=[
                jax.ShapeDtypeStruct((3, fr, width), bf16),
                jax.ShapeDtypeStruct((n_sec,), f32),
                jax.ShapeDtypeStruct((1,), f32),
            ],
            in_specs=[vmem, vmem, vmem, pl.BlockSpec(memory_space=pl.ANY), vmem, vmem, smem, smem, smem],
            out_specs=[vmem, smem, smem],
            scratch_shapes=[
                pltpu.VMEM((2, chans, 128), bf16),
                pltpu.VMEM((samples + 16, 128), f32),
                pltpu.VMEM((samples + 16, 128), f32),
                pltpu.VMEM((width // 128, per_group * taps, 128), f32),
                pltpu.VMEM((taps * chans, width), bf16),
                pltpu.VMEM((fr, taps * chans), bf16),
                pltpu.VMEM((3, n_mp * width, width), bf16),
                pltpu.VMEM((n_mp, fr, width), bf16),
                pltpu.VMEM((n_seq, fr, cols), bf16),
                pltpu.VMEM((n_seq, fr, cols), bf16),
                pltpu.VMEM((3, n_seq, fr, cols), bf16),
                pltpu.VMEM((3, n_seq, fr, cols), bf16),
                pltpu.VMEM((heads, total, total), f32),
                pltpu.VMEM((heads, cols, total), bf16),
                pltpu.VMEM((heads, total, cols), bf16),
                pltpu.VMEM((8, total), f32),
                pltpu.VMEM((cols, total), f32),
                pltpu.VMEM((n_seq * n_mp * n_sec, 8, 128), f32),
                pltpu.VMEM((3, n_seq, fr, cols), bf16),
                dma((2, 2)),
                dma((2, 1)),
                dma,
                dma((2, n_seq)),
                dma((3, 2, n_seq)),
                dma((2, n_seq * n_mp * n_sec)),
                dma((3, 2, n_seq)),
            ],
            compiler_params=pltpu.CompilerParams(
                collective_id=0, has_side_effects=True, vmem_limit_bytes=56 * 2**20
            ),
        )(
            features[0],
            alpha[None, :],
            conv_weight.transpose(1, 2, 0),
            qkv_weight.transpose(1, 0, 2),
            readout.reshape(n_seq, cols),
            freqs,
            offsets,
            pairs,
            labels,
        )
        return grads[:, None], rewards, loss

    return run


def chosen_local(mesh):
    n_seq, n_mp, n_sec = (mesh.shape[axis] for axis in ("seq", "mp", "section"))
    if n_mp == 2 and n_sec == 2 and n_mp * n_seq * 128 == D:
        return fused_local(n_seq, n_mp, n_sec)
    return local


def solution(mesh):
    placed = (
        P(("groups", "section"), "mp", "seq"),
        P("mp"),
        P("mp", None, None),
        P(None, None, "mp"),
        P("mp"),
        P(("groups", "section")),
        P("groups", None),
        P("groups"),
    )
    return jax.shard_map(
        chosen_local(mesh),
        mesh=mesh,
        in_specs=placed,
        out_specs=(P(None, ("groups", "section"), "seq", "mp"), P("groups"), P("groups")),
        check_vma=False,
    )
```
